128 devices in a mesh: row: 16 (over y, x), col: 8 (over z, core).
Axes of the slice: x: 4, y: 4, z: 4, core: 2. Of those that a mesh axis runs over, the one named last changes fastest.
Arguments:
- features: bfloat16 [32768, 256], P(('row', 'col')), may hold values from -6 to 6
- out_degree: int32 [32768], P('row'), may hold values from 8 to 1024
- in_degree: int32 [32768], P('col'), may hold values from 8 to 1024
- tile_blocks: int32 [16, 8, 2, 128], P('row', 'col'), may hold values from 0 to 31, as said below
- tile_count: int32 [16, 8], P('row', 'col'), may hold values from 16 to 128, as said below
- tile_weights: bfloat16 [16, 8, 128, 128, 128], P('row', 'col'), may hold values from 0 to 4, as said below
- weight: bfloat16 [256, 256], replicated, may hold values from -0.375 to 0.375
- cotangent: bfloat16 [32768, 256], P(('col', 'row')), may hold values from -6 to 6
Outputs:
- hidden: bfloat16 [32768, 256], P(('col', 'row'))
- input_grad: bfloat16 [32768, 256], P(('row', 'col'))
- weight_grad: float32 [256, 256], replicated
The draws below stay inside these ranges and needn't reach their ends.
Inputs may be any that keep to these rules, and one draw needn't show every extreme that they name: `tile_blocks`: entry [r, c, 0, s] is a target block below 32, entry [r, c, 1, s] a source block below 16; the pairs of one device position are distinct. `tile_count`: live tile slots of a device position are its first ones; some position has exactly 128. `tile_weights`: Non-negative edge weights.
All inputs are finite; a program needn't handle non-finite values.
Results may differ from the reference program's by a relative error of at most 0.0067.
Values may be sent and summed in bfloat16 or wider, within the bound.
No kernel may reach another device: no remote copies, remote signals or barrier semaphores. Data moves between devices by JAX's collectives and lax.ppermute only.
A program may use at most 192 MiB of HBM per device.

```python
import jax
import jax.numpy as jnp
from jax import lax

HID = 256
TILE = 128
NODE_DEV = 256
TILE_CAP = 128
NODES = 32768
SRC_BLOCKS = 16
TGT_BLOCKS = 32
N_ROW = 16
N_COL = 8


def draw_tile_blocks(key, part):
    region = TGT_BLOCKS * SRC_BLOCKS

    def one_device(index):
        order = jax.random.permutation(jax.random.fold_in(key, index), region)[:TILE_CAP]
        return jnp.stack([order // SRC_BLOCKS, order % SRC_BLOCKS]).astype(jnp.int32)
    picked = jax.vmap(one_device)(jnp.arange(N_ROW * N_COL))
    return picked.reshape(N_ROW, N_COL, 2, TILE_CAP)


def draw_tile_count(key, part):
    positions = N_ROW * N_COL
    base = jax.random.randint(jax.random.fold_in(key, 11), (positions,), max(1, TILE_CAP // 8), TILE_CAP // 2 + 1)
    busiest = jax.random.randint(jax.random.fold_in(key, 12), (), 0, positions)
    filled = jnp.where(jnp.arange(positions) == busiest, TILE_CAP, base)
    return filled.astype(jnp.int32).reshape(N_ROW, N_COL)


def draw_tile_weights(key, part):
    shape = (N_ROW, N_COL, TILE_CAP, TILE, TILE)
    kept = jax.random.bernoulli(jax.random.fold_in(key, 21), 0.5, shape)
    values = jax.random.uniform(jax.random.fold_in(key, 22), shape, jnp.float32, 0.5, 2.0)
    return jnp.where(kept, values, 0.0).astype(jnp.float32).astype(jnp.bfloat16)


def plant(drawn, key, low, high):
    index_at = [jax.random.randint(jax.random.fold_in(key, axis), (), 0, length) for axis, length in enumerate(drawn.shape)]
    widest = drawn.shape.index(max(drawn.shape))
    next_to = index_at[:widest] + [(index_at[widest] + 1) % drawn.shape[widest]] + index_at[widest + 1:]
    return drawn.at[tuple(index_at)].set(low).at[tuple(next_to)].set(high)


def block_scale(rng, dims, split, low, top_value):
    gain = 1.0
    for position, shards_of in split:
        draws = jax.random.uniform(jax.random.fold_in(jax.random.fold_in(rng, 6), position), (shards_of,), jnp.float32, low / len(split), top_value / len(split))
        gain = gain * jnp.repeat(jnp.exp(draws), dims[position] // shards_of).reshape((-1,) + (1,) * (len(dims) - 1 - position))
    return gain


def scatter_about(key, dims, scale, reach, pieces=(), dtype=jnp.bfloat16):
    gain = block_scale(key, dims, pieces, -0.22, 0.18) if pieces else 1.0
    values = jax.random.normal(key, dims, jnp.float32) * scale * gain
    return jnp.minimum(jnp.maximum(values, -reach), reach).astype(dtype)


def setup_inputs(seed: int = 0) -> dict:
    key_list = jax.random.split(jax.random.key(seed), 9)
    return {
        "features": scatter_about(key_list[0], (NODES, HID), 1.0, 6.0, ((0, 128),)),
        "out_degree": plant(jax.random.randint(key_list[1], (NODES,), 8, 1025), jax.random.fold_in(key_list[1], 1), 8, 1024).astype(jnp.int32),
        "in_degree": plant(jax.random.randint(key_list[2], (NODES,), 8, 1025), jax.random.fold_in(key_list[2], 1), 8, 1024).astype(jnp.int32),
        "tile_blocks": draw_tile_blocks(jax.random.fold_in(key_list[8], 71), 0),
        "tile_count": draw_tile_count(jax.random.fold_in(key_list[8], 71), 0),
        "tile_weights": draw_tile_weights(jax.random.fold_in(key_list[8], 71), 0),
        "weight": scatter_about(key_list[6], (HID, HID), HID ** -0.5, 0.375),
        "cotangent": scatter_about(key_list[7], (NODES, HID), 1.0, 6.0, ((0, 128),)),
    }


def silu_slope(pre_act):
    gate_sig = jax.nn.sigmoid(pre_act)
    return gate_sig * (1.0 + pre_act * (1.0 - gate_sig))

def reference(features, out_degree, in_degree, tile_blocks, tile_count, tile_weights, weight, cotangent):
    feat_width = features.shape[1]
    src_len = NODE_DEV * N_COL
    tgt_len = NODE_DEV * N_ROW
    out_scale = lax.rsqrt(out_degree.astype(jnp.float32))
    in_scale = lax.rsqrt(in_degree.astype(jnp.float32))
    src_scaled = (features.astype(jnp.float32) * out_scale[:, None]).astype(jnp.bfloat16)

    def device_tiles(device_at):
        row_at = (device_at // N_COL).astype(jnp.int32)
        col_at = (device_at % N_COL).astype(jnp.int32)
        blocks = tile_blocks[row_at, col_at]
        is_live = (jnp.arange(TILE_CAP) < tile_count[row_at, col_at]).astype(jnp.float32)
        tile_vals = tile_weights[row_at, col_at].astype(jnp.float32) * is_live[:, None, None]
        return (row_at, col_at, blocks, tile_vals)

    def forward_step(device_at, totals):
        row_at, col_at, blocks, tile_vals = device_tiles(device_at)
        source = lax.dynamic_slice_in_dim(src_scaled, row_at * src_len, src_len, 0)
        source = source.reshape(SRC_BLOCKS, TILE, feat_width)
        picked = source[blocks[1]].astype(jnp.float32)
        products = jnp.einsum('trc,tch->trh', tile_vals, picked)
        partial_value = jax.ops.segment_sum(products, blocks[0], num_segments=TGT_BLOCKS)
        return totals.at[col_at].add(partial_value.reshape(tgt_len, feat_width))
    totals = lax.fori_loop(0, N_ROW * N_COL, forward_step, jnp.zeros((N_COL, tgt_len, feat_width), jnp.float32))
    agg_rows = (totals.reshape(NODES, feat_width) * in_scale[:, None]).astype(jnp.bfloat16)
    pre_act = jnp.dot(agg_rows, weight, preferred_element_type=jnp.float32)
    hidden = jax.nn.silu(pre_act).astype(jnp.bfloat16)
    pre_grad = (cotangent.astype(jnp.float32) * silu_slope(pre_act)).astype(jnp.bfloat16)
    weight_grad = jnp.dot(agg_rows.T, pre_grad, preferred_element_type=jnp.float32)
    back_rows = jnp.dot(pre_grad, weight.T, preferred_element_type=jnp.float32)
    target_grad = (back_rows * in_scale[:, None]).astype(jnp.bfloat16)

    def backward_step(device_at, totals):
        row_at, col_at, blocks, tile_vals = device_tiles(device_at)
        target = lax.dynamic_slice_in_dim(target_grad, col_at * tgt_len, tgt_len, 0)
        target = target.reshape(TGT_BLOCKS, TILE, feat_width)
        picked = target[blocks[0]].astype(jnp.float32)
        products = jnp.einsum('trc,trh->tch', tile_vals, picked)
        partial_value = jax.ops.segment_sum(products, blocks[1], num_segments=SRC_BLOCKS)
        return totals.at[row_at].add(partial_value.reshape(src_len, feat_width))
    src_totals = lax.fori_loop(0, N_ROW * N_COL, backward_step, jnp.zeros((N_ROW, src_len, feat_width), jnp.float32))
    input_grad = (src_totals.reshape(NODES, feat_width) * out_scale[:, None]).astype(jnp.bfloat16)
    return (hidden, input_grad, weight_grad)
```

```python
import functools

import jax
import jax.numpy as jnp
from jax import lax
from jax.experimental import pallas as pl
from jax.experimental.pallas import tpu as pltpu
from jax.sharding import PartitionSpec as P

TILE = 128
HID = 256
UNROLL = 8
CHUNK = 16
F32 = jnp.float32
BF16 = jnp.bfloat16
SMEM = pl.BlockSpec(memory_space=pltpu.SMEM)
VMEM = pl.BlockSpec(memory_space=pltpu.VMEM)
ANY = pl.BlockSpec(memory_space=pl.ANY)


def row_pairs(dy, dx):
    return [
        (y * 4 + x, (y + dy) % 4 * 4 + (x + dx) % 4) for y in range(4) for x in range(4)
    ]


def col_pairs(dz, dk):
    return [
        (z * 2 + k, (z + dz) % 4 * 2 + (k + dk) % 2) for z in range(4) for k in range(2)
    ]


def send_y(array, step):
    return lax.ppermute(array, "row", row_pairs(step, 0))


def send_x(array, step):
    return lax.ppermute(array, "row", row_pairs(0, step))


def send_z(array, step):
    return lax.ppermute(array, "col", col_pairs(step, 0))


def send_core(array):
    return lax.ppermute(array, "col", col_pairs(0, 1))


def shape(rows, dtype, cols=HID):
    return jax.ShapeDtypeStruct((rows, cols), dtype)


def call(kernel, name, outs, ins, args, scratch=(), aliases=None, out_specs=None):
    return pl.pallas_call(
        kernel,
        name=name,
        out_shape=tuple(outs),
        in_specs=list(ins),
        out_specs=tuple(out_specs or [VMEM] * len(outs)),
        scratch_shapes=list(scratch),
        input_output_aliases=aliases or {},
    )(*args)


def column_scale(degree_row):
    scale = lax.rsqrt(degree_row.astype(F32))
    square = jnp.transpose(jnp.broadcast_to(scale, (TILE, TILE)))
    return jnp.concatenate([square, square], axis=1)


def dot(lhs, rhs, lhs_dim, rhs_dim):
    return lax.dot_general(
        lhs, rhs, (((lhs_dim,), (rhs_dim,)), ((), ())), preferred_element_type=F32
    )


def scale_kernel(features, out_degree, scaled):
    col_at = lax.axis_index("col")
    for half in range(2):
        rows = pl.ds(half * TILE, TILE)
        scale = column_scale(out_degree[pl.ds(2 * col_at + half, 1), :])
        scaled[rows, :] = (features[rows, :].astype(F32) * scale).astype(BF16)


def prep_kernel(blocks, count, weights_hbm, lists, sizes, weights, sems):
    row_at = lax.axis_index("row")
    col_at = lax.axis_index("col")
    y_at, x_at = row_at // 4, row_at % 4
    z_at, k_at = col_at // 2, col_at % 2
    live = count[0, 0]

    def copy(at):
        part = pl.ds(at * CHUNK, CHUNK)
        return pltpu.make_async_copy(weights_hbm.at[part], weights.at[part], sems.at[at])

    chunks = weights.shape[0] // CHUNK
    for at in range(chunks):
        pl.when(at * CHUNK < live)(copy(at).start)

    def one(slot, filled):
        tgt, src = blocks[0, slot], blocks[1, slot]
        odd = tgt & 1
        y_of, x_of = tgt >> 3, (tgt >> 1) & 3
        z_of, k_of, half = src >> 2, (src >> 1) & 1, src & 1
        dk = (k_of - k_at) & 1
        dy, dx, dz = (y_of - y_at) & 3, (x_of - x_at) & 3, (z_of - z_at) & 3
        ry, rx, rz = (4 - dy) & 3, (4 - dx) & 3, (4 - dz) & 3
        fwd_dst = jnp.where(odd == 0, dy * 4 + dx, dx * 4 + dy)
        bwd_src = jnp.where(odd == 0, ry * 4 + rx, rx * 4 + ry)
        fwd_src = (dk * 4 + rz) * 2 + half
        bwd_dst = (dk * 4 + dz) * 2 + half
        packed = slot + fwd_src * 128 + bwd_src * 2048 + fwd_dst * 32768 + bwd_dst * 1048576
        at = jnp.where(odd == 0, filled[0], filled[1])
        lists[odd, at] = packed
        return filled[0] + 1 - odd, filled[1] + odd

    sizes_now = lax.fori_loop(0, live, one, (jnp.int32(0), jnp.int32(0)))
    for odd in range(2):
        sizes[odd] = sizes_now[odd]
        for extra in range(UNROLL):
            lists[odd, sizes_now[odd] + extra] = 16 * 32768 + 16 * 1048576
    for at in range(chunks):
        pl.when(at * CHUNK < live)(copy(at).wait)


def run_tiles(lists, sizes, odd, weights, inputs, sums, transpose):
    def step(at, carry):
        first = at * UNROLL
        items = [lists[odd, first + k] for k in range(UNROLL)]
        products = []
        for item in items:
            tile = weights[item & 127]
            if transpose:
                products.append(dot(tile, inputs[(item >> 11) & 15], 0, 0))
            else:
                products.append(dot(tile, inputs[(item >> 7) & 15], 1, 0))
        for item, product in zip(items, products):
            where = (item >> 20) & 31 if transpose else (item >> 15) & 31
            sums[where] += product
        return carry

    lax.fori_loop(0, (sizes[odd] + UNROLL - 1) // UNROLL, step, 0)


def fwd_kernel(odd, lists, sizes, weights, *refs):
    if odd == 0:
        sources, outs, inputs, sums = refs[:8], refs[8:12], refs[12], refs[13]
        for at, ref in enumerate(sources):
            inputs[2 * at] = ref[:TILE, :]
            inputs[2 * at + 1] = ref[TILE:, :]
    else:
        inputs, outs, sums = refs[0], refs[1:5], refs[5]
    sums[...] = jnp.zeros_like(sums)
    run_tiles(lists, sizes, odd, weights, inputs, sums, False)
    for at in range(4):
        part = sums[pl.ds(4 * at, 4)].reshape(4 * TILE, HID)
        outs[at][...] = part.astype(outs[at].dtype)


def sum_kernel(parts, *refs):
    own, others, outs = refs[0], refs[1:-parts], refs[-parts:]
    rows = own.shape[0] // parts
    for at in range(parts):
        part = pl.ds(at * rows, rows)
        total = own[part, :].astype(F32)
        for other in others:
            total = total + other[part, :].astype(F32)
        outs[at][...] = total.astype(outs[at].dtype)


def node_kernel(odd, own, one, two, three, in_degree, weight, cotangent, *refs):
    if odd:
        hidden_in, weight_in, hidden, target_grad, *weight_outs, weight_sum = refs
    else:
        hidden, target_grad, weight_sum = refs
    row_at = lax.axis_index("row")
    rows = pl.ds(odd * TILE, TILE)
    scale = column_scale(in_degree[pl.ds(2 * row_at + odd, 1), :])
    total = own[...] + one[...].astype(F32) + two[...].astype(F32) + three[...].astype(F32)
    aggregated = (total * scale).astype(BF16)
    pre_act = dot(aggregated, weight[...], 1, 0)
    gate = jax.nn.sigmoid(pre_act)
    hidden[rows, :] = (pre_act * gate).astype(BF16)
    slope = gate * (1.0 + pre_act * (1.0 - gate))
    pre_grad = (cotangent[rows, :].astype(F32) * slope).astype(BF16)
    back = dot(pre_grad, weight[...], 1, 1)
    target_grad[...] = (back * scale).astype(BF16)
    part = dot(aggregated, pre_grad, 0, 0)
    if odd:
        hidden[pl.ds(0, TILE), :] = hidden_in[pl.ds(0, TILE), :]
        weight_sum[...] = part + weight_in[...]
        x_at = row_at % 4
        for step in range(4):
            first = pl.multiple_of((x_at + step) % 4 * 64, 64)
            weight_outs[step][...] = weight_sum[pl.ds(first, 64), :]
    else:
        weight_sum[...] = part


def join_kernel(*refs):
    out = refs[-1]
    for at, ref in enumerate(refs[:-1]):
        out[pl.ds(at * ref.shape[0], ref.shape[0]), :] = ref[...]


def bwd_kernel(odd, lists, sizes, weights, *refs):
    grads, refs = refs[:4], refs[4:]
    if odd:
        sums_in, own, other, inputs, sums = refs
        sums[...] = sums_in[...]
    else:
        sums, inputs = refs
        sums[...] = jnp.zeros_like(sums)
    for at, ref in enumerate(grads):
        inputs[pl.ds(4 * at, 4)] = ref[...].reshape(4, TILE, HID)
    run_tiles(lists, sizes, odd, weights, inputs, sums, True)
    if odd:
        own[...] = sums[pl.ds(0, 8)].reshape(8 * TILE, HID)
        other[...] = sums[pl.ds(8, 8)].reshape(8 * TILE, HID).astype(BF16)


def final_kernel(own, one, two, three, out_degree, input_grad):
    col_at = lax.axis_index("col")
    for half in range(2):
        rows = pl.ds(half * TILE, TILE)
        scale = column_scale(out_degree[pl.ds(2 * col_at + half, 1), :])
        total = own[rows, :]
        for ref in (one, two, three):
            total = total + ref[rows, :].astype(F32)
        input_grad[rows, :] = (total * scale).astype(BF16)


def weight_y_kernel(own, one, two, three, *refs):
    outs, total = refs[:4], refs[4]
    y_at = lax.axis_index("row") // 4
    total[...] = own[...] + one[...] + two[...] + three[...]
    for step in range(4):
        first = pl.multiple_of((y_at + step) % 4 * 16, 16)
        outs[step][...] = total[pl.ds(first, 16), :]


def weight_join_kernel(own, one, two, three, out):
    y_at = lax.axis_index("row") // 4
    for step, ref in enumerate((own, one, two, three)):
        first = pl.multiple_of((y_at - step + 4) % 4 * 16, 16)
        out[pl.ds(first, 16), :] = ref[...]


def weight_out_kernel(own, one, two, three, out):
    x_at = lax.axis_index("row") % 4
    for step, ref in enumerate((own, one, two, three)):
        first = pl.multiple_of((x_at - step + 4) % 4 * 64, 64)
        out[pl.ds(first, 64), :] = ref[...]


def shards(
    features, out_degree, in_degree, tile_blocks, tile_count, tile_weights, weight, cotangent
):
    slots = tile_weights.shape[2]
    out_rows = out_degree.reshape(-1, TILE)
    in_rows = in_degree.reshape(-1, TILE)
    steps = (1, 2, 3)

    (scaled,) = call(
        scale_kernel, "scale", [shape(HID, BF16)], [VMEM, VMEM], (features, out_rows)
    )
    z_parts = [scaled] + [send_z(scaled, step) for step in steps]
    lists, sizes, weights = call(
        prep_kernel,
        "prep",
        [
            jax.ShapeDtypeStruct((2, slots + UNROLL), jnp.int32),
            jax.ShapeDtypeStruct((2,), jnp.int32),
            jax.ShapeDtypeStruct((slots, TILE, TILE), BF16),
        ],
        [SMEM, SMEM, ANY],
        (tile_blocks[0, 0], tile_count, tile_weights[0, 0]),
        scratch=[pltpu.SemaphoreType.DMA((slots // CHUNK,))],
        out_specs=[SMEM, SMEM, VMEM],
    )
    sources = z_parts + [send_core(part) for part in z_parts]

    stack = jax.ShapeDtypeStruct((16, TILE, HID), BF16)
    sums_shape = pltpu.VMEM((17, TILE, HID), F32)
    partial = [shape(4 * TILE, F32)] + [shape(4 * TILE, BF16)] * 3
    *even_parts, inputs = call(
        functools.partial(fwd_kernel, 0),
        "fwd_even",
        partial + [stack],
        [SMEM, SMEM, VMEM] + [VMEM] * 8,
        (lists, sizes, weights, *sources),
        scratch=[sums_shape],
    )
    even_got = [send_y(part, step) for part, step in zip(even_parts[1:], steps)]
    odd_parts = call(
        functools.partial(fwd_kernel, 1),
        "fwd_odd",
        partial,
        [SMEM, SMEM, VMEM, VMEM],
        (lists, sizes, weights, inputs),
        scratch=[sums_shape],
    )
    odd_got = [send_x(part, step) for part, step in zip(odd_parts[1:], steps)]

    quarter = [shape(TILE, F32)] + [shape(TILE, BF16)] * 3

    def sum_four(name, own, got, outs):
        return call(
            functools.partial(sum_kernel, len(outs)),
            name,
            outs,
            [VMEM] * (1 + len(got)),
            (own, *got),
        )

    even_sums = sum_four("sum_even", even_parts[0], even_got, quarter)
    even_last = [send_x(part, step) for part, step in zip(even_sums[1:], steps)]
    odd_sums = sum_four("sum_odd", odd_parts[0], odd_got, quarter)
    odd_last = [send_y(part, step) for part, step in zip(odd_sums[1:], steps)]

    hidden, even_grad, weight_part = call(
        functools.partial(node_kernel, 0),
        "node_even",
        [shape(HID, BF16), shape(TILE, BF16), shape(HID, F32)],
        [VMEM] * 7,
        (even_sums[0], *even_last, in_rows, weight, cotangent),
    )
    even_near = [send_x(even_grad, step) for step in steps]
    hidden, odd_grad, *weight_parts = call(
        functools.partial(node_kernel, 1),
        "node_odd",
        [shape(HID, BF16), shape(TILE, BF16)] + [shape(64, F32)] * 4,
        [VMEM] * 9,
        (odd_sums[0], *odd_last, in_rows, weight, cotangent, hidden, weight_part),
        scratch=[pltpu.VMEM((HID, HID), F32)],
    )
    odd_near = [send_y(odd_grad, step) for step in steps]

    def join(name, parts):
        (joined,) = call(
            join_kernel, name, [shape(4 * TILE, BF16)], [VMEM] * 4, tuple(parts)
        )
        return joined

    even_group = join("join_even", [even_grad] + even_near)
    even_all = [even_group] + [send_y(even_group, step) for step in steps]
    odd_group = join("join_odd", [odd_grad] + odd_near)
    odd_all = [odd_group] + [send_x(odd_group, step) for step in steps]

    weight_got = [send_x(part, step) for part, step in zip(weight_parts[1:], steps)]
    weight_parts = call(
        weight_y_kernel,
        "weight_y",
        [shape(16, F32)] * 4,
        [VMEM] * 4,
        (weight_parts[0], *weight_got),
        scratch=[pltpu.VMEM((64, HID), F32)],
    )
    weight_got = [send_y(part, step) for part, step in zip(weight_parts[1:], steps)]
    (piece,) = sum_four("weight_z", weight_parts[0], weight_got, [shape(16, F32)])
    weight_got = [send_z(piece, step) for step in steps]
    (piece,) = sum_four("weight_core", piece, weight_got, [shape(16, F32)])
    weight_got = [send_core(piece)]
    (piece,) = sum_four("weight_sum", piece, weight_got, [shape(16, F32)])
    weight_got = [send_y(piece, step) for step in steps]
    (piece,) = call(
        weight_join_kernel, "weight_join", [shape(64, F32)], [VMEM] * 4, (piece, *weight_got)
    )
    weight_got = [send_x(piece, step) for step in steps]
    (weight_grad,) = call(
        weight_out_kernel, "weight_out", [shape(HID, F32)], [VMEM] * 4, (piece, *weight_got)
    )

    (back_sums,) = call(
        functools.partial(bwd_kernel, 0),
        "bwd_even",
        [jax.ShapeDtypeStruct((17, TILE, HID), F32)],
        [SMEM, SMEM, VMEM] + [VMEM] * 4,
        (lists, sizes, weights, *even_all),
        scratch=[pltpu.VMEM((16, TILE, HID), BF16)],
    )
    own_core, other_core = call(
        functools.partial(bwd_kernel, 1),
        "bwd_odd",
        [shape(8 * TILE, F32), shape(8 * TILE, BF16)],
        [SMEM, SMEM, VMEM] + [VMEM] * 5,
        (lists, sizes, weights, *odd_all, back_sums),
        scratch=[pltpu.VMEM((16, TILE, HID), BF16), sums_shape],
    )
    core_got = send_core(other_core)
    back = sum_four(
        "sum_core", own_core, [core_got], [shape(HID, F32)] + [shape(HID, BF16)] * 3
    )
    back_got = [send_z(part, step) for part, step in zip(back[1:], steps)]
    (input_grad,) = call(
        final_kernel, "final", [shape(HID, BF16)], [VMEM] * 5, (back[0], *back_got, out_rows)
    )
    return (hidden, input_grad, weight_grad)


def solution(mesh):
    placed = (
        P(("row", "col"), None),
        P("row"),
        P("col"),
        P("row", "col", None, None),
        P("row", "col"),
        P("row", "col", None, None, None),
        P(),
        P(("col", "row"), None),
    )
    return jax.shard_map(
        shards,
        mesh=mesh,
        in_specs=placed,
        out_specs=(P(("col", "row"), None), P(("row", "col"), None), P()),
        check_vma=False,
    )
```
